32 devices in a mesh: row: 4 (over x, core), col: 8 (over z, y).
Axes of the slice: x: 2, y: 2, z: 4, core: 2. Of those that a mesh axis runs over, the one named last changes fastest.
Arguments:
- tile_list: int32 [512, 2], P(('row', 'col')), may hold values from -1 to 63, as said below
- tile_values: bfloat16 [512, 512, 512], P(('row', 'col'))
- block_order: int32 [64], replicated, may hold values from 0 to 63, as said below
- basis: bfloat16 [64, 512, 256], P(('row', 'col')), may hold values from -8 to 8
Outputs:
- basis_out: bfloat16 [64, 512, 256], P(('row', 'col'))
- projected: float32 [256, 256], replicated
The draws below stay inside these ranges and needn't reach their ends.
Inputs may be any that keep to these rules, and one draw needn't show every extreme that they name: `block_order`: A permutation of the channel blocks; slot p lies on device p // 2 in row-major order of (row, col). `tile_list`: slots of device (i, j) hold tiles whose row block sits in a slot of a device of row index i and whose column block sits in a slot of a device of column index j; each unordered pair of blocks appears at most once in all; empty slots hold -1 in both columns and may stand anywhere among a device's slots; every device holds at most 16 tiles and some device holds exactly 16.
All inputs are finite; a program needn't handle non-finite values.
Results may differ from the reference program's by a relative error of at most 0.0017.
Values may be sent and summed in bfloat16 or wider, within the bound.
A program may use at most 128 MiB of HBM per device.

```python
import jax
import jax.numpy as jnp
from jax import lax

B = 512
K = 256
BLK_DEV = 2
TPD = 16
ROW_GROUP = 16
COL_GROUP = 8
NB = 64
N = 32768
SLOTS = 512


def make_plan(key):
    base = jax.random.fold_in(key, 9173)
    order_key, score_key, count_key = jax.random.split(base, 3)
    order = jax.random.permutation(order_key, NB).astype(jnp.int32)
    col_count = ROW_GROUP // BLK_DEV
    device_count = NB // BLK_DEV
    devices = jnp.arange(device_count, dtype=jnp.int32)
    row_index = devices // col_count
    col_index = devices % col_count
    row_slots = row_index[:, None] * ROW_GROUP + jnp.arange(ROW_GROUP, dtype=jnp.int32)[None, :]
    group_pos = jnp.arange(COL_GROUP, dtype=jnp.int32)
    col_slots = ((group_pos // BLK_DEV)[None, :] * col_count + col_index[:, None]) * BLK_DEV + (group_pos % BLK_DEV)[None, :]
    first_block = jnp.broadcast_to(order[row_slots][:, :, None], (device_count, ROW_GROUP, COL_GROUP))
    second_block = jnp.broadcast_to(order[col_slots][:, None, :], (device_count, ROW_GROUP, COL_GROUP))
    odd_sum = (first_block + second_block) % 2 == 1
    canon = (first_block == second_block) | ((first_block < second_block) != odd_sum)
    cand = ROW_GROUP * COL_GROUP
    canon = canon.reshape(device_count, cand)
    first_flat = first_block.reshape(device_count, cand)
    second_flat = second_block.reshape(device_count, cand)
    index_row = jnp.arange(cand, dtype=jnp.int32)[None, :]
    noise = jax.random.randint(score_key, (device_count, cand), 0, 65536, dtype=jnp.int32)
    score = jnp.where(canon, noise * cand + index_row, -1 - index_row)
    _, picked = lax.top_k(score, TPD)
    canon_count = jnp.sum(canon.astype(jnp.int32), axis=1)
    counts = jax.random.randint(count_key, (device_count,), TPD // 4, TPD + 1, dtype=jnp.int32)
    fullest = jnp.argmax(canon_count)
    counts = counts.at[fullest].set(TPD)
    counts = jnp.minimum(counts, canon_count)
    live = jnp.arange(TPD, dtype=jnp.int32)[None, :] < counts[:, None]
    first_pick = jnp.take_along_axis(first_flat, picked, axis=1)
    second_pick = jnp.take_along_axis(second_flat, picked, axis=1)
    tiles = jnp.stack([jnp.where(live, first_pick, -1), jnp.where(live, second_pick, -1)], axis=-1)
    return (order, tiles.reshape(SLOTS, 2).astype(jnp.int32))


def draw_block_order(key, part):
    order, _ = make_plan(key)
    return order


def draw_tile_list(key, part):
    _, tiles = make_plan(key)
    return tiles


def draw_tile_values(key, part):
    value_key = jax.random.fold_in(key, 4421)
    sigma = (B * TPD / BLK_DEV) ** (-0.5)
    values = jax.random.normal(value_key, (SLOTS, B, B), jnp.float32) * sigma
    return values.astype(jnp.bfloat16)


def draw_basis(key, part):
    basis_key = jax.random.fold_in(key, 6607)
    leading_key, partner_key, column_key = jax.random.split(basis_key, 3)
    half_rank = K // 2
    ladder = jnp.arange(half_rank, dtype=jnp.float32) / (half_rank - 1)
    offsets = 0.004 * jnp.exp(ladder * 4.317488)
    leading = jnp.clip(jax.random.normal(leading_key, (NB, B, half_rank), jnp.float32), -5.0, 5.0)
    partner_noise = jnp.clip(jax.random.normal(partner_key, (NB, B, half_rank), jnp.float32), -5.0, 5.0)
    partner = leading + offsets * partner_noise
    paired = jnp.stack([leading, partner], axis=3).reshape(NB, B, K)
    column_order = jax.random.permutation(column_key, K).astype(jnp.int32)
    return jnp.take(paired, column_order, axis=2).astype(jnp.bfloat16)


def setup_inputs(seed: int = 0) -> dict:
    seeds = jax.random.split(jax.random.key(seed), 5)
    tile_list = draw_tile_list(jax.random.fold_in(seeds[4], 71), 0)
    tile_values = draw_tile_values(jax.random.fold_in(seeds[4], 71), 0)
    block_order = draw_block_order(jax.random.fold_in(seeds[4], 71), 0)
    basis = draw_basis(jax.random.fold_in(seeds[4], 71), 0)
    return {"tile_list": tile_list, "tile_values": tile_values, "block_order": block_order, "basis": basis}


def reference(tile_list, tile_values, block_order, basis):
    slot_of = jnp.zeros((NB,), jnp.int32).at[block_order].set(jnp.arange(NB, dtype=jnp.int32))
    present = tile_list[:, 0] >= 0
    first_slot = slot_of[jnp.where(present, tile_list[:, 0], 0)].astype(jnp.int32)
    second_slot = slot_of[jnp.where(present, tile_list[:, 1], 0)].astype(jnp.int32)

    def add_tile(total, item):
        tile, first, second, live = item
        weight = jnp.where(live, 1.0, 0.0).astype(jnp.float32)
        near = jnp.dot(tile.astype(jnp.float32), basis[second].astype(jnp.float32), preferred_element_type=jnp.float32) * weight
        far = jnp.dot(tile.T.astype(jnp.float32), basis[first].astype(jnp.float32), preferred_element_type=jnp.float32) * weight
        total = total.at[first].add(near)
        total = total.at[second].add(far)
        return (total, None)
    start = jnp.zeros((NB, B, K), jnp.float32)
    product, _ = lax.scan(add_tile, start, (tile_values, first_slot, second_slot, present))
    flat = product.reshape(N, K)
    scale = jnp.sqrt(jnp.float32(N))
    old = basis.reshape(N, K).astype(jnp.float32)
    projected = jnp.dot(old.T, flat, precision=lax.Precision.HIGHEST) / scale
    gram = jnp.dot(flat.T, flat, precision=lax.Precision.HIGHEST)
    first_factor = jnp.linalg.cholesky(gram)
    first_basis = lax.linalg.triangular_solve(first_factor, flat, left_side=False, lower=True, transpose_a=True)
    second = jnp.dot(first_basis.T, first_basis, precision=lax.Precision.HIGHEST)
    second_factor = jnp.linalg.cholesky(second)
    final = lax.linalg.triangular_solve(second_factor, first_basis, left_side=False, lower=True, transpose_a=True)
    basis_out = (final * scale).astype(jnp.bfloat16).reshape(NB, B, K)
    return (basis_out, projected)
```

```python
import functools

import jax
import jax.numpy as jnp
from jax import lax
from jax.experimental import pallas as pl
from jax.experimental.pallas import tpu as pltpu
from jax.sharding import PartitionSpec as P

MESH = pl.DeviceIdType.MESH
HIGHEST = lax.Precision.HIGHEST
VMEM_MAX = 67043328


def tile_kernel(row_local, col_local, tile_ref, col_side, row_side, row_out, col_out):
    t = pl.program_id(0)

    @pl.when(t == 0)
    def _():
        @pl.loop(0, row_out.shape[0])
        def _(i):
            row_out[i] = jnp.zeros(row_out.shape[1:], jnp.float32)

        @pl.loop(0, col_out.shape[0])
        def _(i):
            col_out[i] = jnp.zeros(col_out.shape[1:], jnp.float32)

    r = row_local[t]
    c = col_local[t]

    @pl.when(r >= 0)
    def _():
        tile = tile_ref[0]
        row_out[r] += jnp.dot(tile, col_side[c], preferred_element_type=jnp.float32)
        col_out[c] += lax.dot_general(
            tile, row_side[r], (((0,), (0,)), ((), ())), preferred_element_type=jnp.float32
        )


def tile_products(row_local, col_local, tiles, col_side, row_side):
    count, edge, _ = tiles.shape
    rank = col_side.shape[2]
    rows, cols = row_side.shape[0], col_side.shape[0]

    def whole(n):
        return pl.BlockSpec(
            (n, edge, rank), lambda t, *_: (0, 0, 0), pipeline_mode=pl.Buffered(1)
        )

    return pl.pallas_call(
        tile_kernel,
        grid_spec=pltpu.PrefetchScalarGridSpec(
            num_scalar_prefetch=2,
            grid=(count,),
            in_specs=[
                pl.BlockSpec((1, edge, edge), lambda t, *_: (t, 0, 0)),
                whole(cols),
                whole(rows),
            ],
            out_specs=[whole(rows), whole(cols)],
        ),
        out_shape=[
            jax.ShapeDtypeStruct((rows, edge, rank), jnp.float32),
            jax.ShapeDtypeStruct((cols, edge, rank), jnp.float32),
        ],
        compiler_params=pltpu.CompilerParams(vmem_limit_bytes=VMEM_MAX),
        name="tile_products",
    )(row_local, col_local, tiles, col_side, row_side)


def sum_kernel(nr, nc, x_ref, out_ref, land_row, mid, land_col, send_sem, recv_sem):
    r = lax.axis_index("row")
    c = lax.axis_index("col")

    def row_peer(o):
        return lax.rem(r + o, nr)

    def col_peer(o):
        return lax.rem(c + o, nc)

    barrier = pltpu.get_barrier_semaphore()
    for o in range(1, nr):
        pl.semaphore_signal(barrier, inc=1, device_id=(row_peer(o), c), device_id_type=MESH)
    for o in range(1, nc):
        pl.semaphore_signal(barrier, inc=1, device_id=(r, col_peer(o)), device_id_type=MESH)
    pl.semaphore_wait(barrier, nr + nc - 2)

    def copy(src, dst, sem, device):
        return pltpu.make_async_remote_copy(
            src_ref=src,
            dst_ref=dst,
            send_sem=send_sem.at[sem],
            recv_sem=recv_sem.at[sem],
            device_id=device,
            device_id_type=MESH,
        )

    base = 0
    copies = []
    for o in range(1, nr):
        p = row_peer(o)
        copies.append(copy(x_ref.at[p], land_row.at[o - 1], base + o - 1, (p, c)))
    for k in copies:
        k.start()
    total = x_ref[r]
    for o, k in enumerate(copies):
        k.wait_recv()
        total += land_row[o]
    mid[...] = total
    sent = copies

    base += nr - 1
    copies = []
    for o in range(1, nc):
        p = col_peer(o)
        copies.append(copy(mid.at[p], land_col.at[o - 1], base + o - 1, (r, p)))
    for k in copies:
        k.start()
    total = mid[c]
    for o, k in enumerate(copies):
        k.wait_recv()
        total += land_col[o]
    out_ref[r, c] = total
    sent = sent + copies

    base += nc - 1
    copies = []
    for o in range(1, nc):
        p = col_peer(o)
        copies.append(copy(out_ref.at[r, c], out_ref.at[r, c], base + o - 1, (r, p)))
    for k in copies:
        k.start()
    for k in copies:
        k.wait_recv()
    sent = sent + copies

    base += nc - 1
    copies = []
    for o in range(1, nr):
        p = row_peer(o)
        copies.append(copy(out_ref.at[r], out_ref.at[r], base + o - 1, (p, c)))
    for k in copies:
        k.start()
    for k in copies:
        k.wait_recv()
    for k in sent + copies:
        k.wait_send()


def sum_all(x, collective_id):
    nr, nc = lax.axis_size("row"), lax.axis_size("col")
    rows, rank = x.shape
    part = rows // (nr * nc)
    sems = 2 * (nr + nc - 2)
    y = pl.pallas_call(
        functools.partial(sum_kernel, nr, nc),
        out_shape=jax.ShapeDtypeStruct((nr, nc, part, rank), jnp.float32),
        in_specs=[pl.BlockSpec(memory_space=pltpu.VMEM)],
        out_specs=pl.BlockSpec(memory_space=pltpu.VMEM),
        scratch_shapes=[
            pltpu.VMEM((nr - 1, nc, part, rank), jnp.float32),
            pltpu.VMEM((nc, part, rank), jnp.float32),
            pltpu.VMEM((nc - 1, part, rank), jnp.float32),
            pltpu.SemaphoreType.DMA((sems,)),
            pltpu.SemaphoreType.DMA((sems,)),
        ],
        compiler_params=pltpu.CompilerParams(collective_id=collective_id, has_side_effects=True),
        name="sum_all",
    )(x.reshape(nr, nc, part, rank))
    return y.reshape(rows, rank)


def invert_panel(x):
    n = x.shape[0]
    rows = lax.broadcasted_iota(jnp.int32, (n, n), 0)
    cols = lax.broadcasted_iota(jnp.int32, (n, n), 1)
    pivots = jnp.ones((n, n), jnp.float32)
    for j in range(n):
        column = jnp.broadcast_to(x[:, j : j + 1], (n, n))
        pivot = jnp.broadcast_to(column[j : j + 1, :], (n, n))
        line = jnp.broadcast_to(x[j : j + 1, :], (n, n))
        line = jnp.where(cols == j, 1.0, line)
        pivots = jnp.where(rows == j, pivot, pivots)
        base = jnp.where(cols == j, 0.0, x)
        x = jnp.where(rows > j, base - (column / pivot) * line, x)
    x = jnp.where(rows == cols, 1.0, jnp.where(rows > cols, x, 0.0))
    return x * lax.rsqrt(pivots)


def inverse_kernel(panel, a_ref, out_ref):
    rank = a_ref.shape[0]
    out_ref[...] = a_ref[...]
    for k in range(rank // panel):
        lo, hi = k * panel, (k + 1) * panel
        inv = invert_panel(out_ref[lo:hi, lo:hi])
        out_ref[lo:hi, lo:hi] = inv
        strip = out_ref[lo:hi, :]
        cols = lax.broadcasted_iota(jnp.int32, strip.shape, 1)
        new = jnp.dot(inv, strip, precision=HIGHEST, preferred_element_type=jnp.float32)
        done = jnp.where((cols >= lo) & (cols < hi), strip, new)
        out_ref[lo:hi, :] = jnp.where(cols < hi, done, 0.0)
        if hi < rank:
            out_ref[hi:, lo:hi] = jnp.zeros((rank - hi, panel), jnp.float32)
            out_ref[hi:, :] -= lax.dot_general(
                new,
                done,
                (((0,), (0,)), ((), ())),
                precision=HIGHEST,
                preferred_element_type=jnp.float32,
            )[hi:, :]


def inverse_factor(a):
    return pl.pallas_call(
        functools.partial(inverse_kernel, 32),
        out_shape=jax.ShapeDtypeStruct(a.shape, jnp.float32),
        in_specs=[pl.BlockSpec(memory_space=pltpu.VMEM)],
        out_specs=pl.BlockSpec(memory_space=pltpu.VMEM),
        name="inverse_factor",
    )(a)


def times_transposed(x, m):
    return lax.dot_general(x, m, (((1,), (1,)), ((), ())), precision=HIGHEST)


def gram_of(x, y):
    return lax.dot_general(x, y, (((0,), (0,)), ((), ())), precision=HIGHEST)


def per_device(tile_list, tile_values, block_order, basis):
    rows_count = lax.axis_size("row")
    cols_count = lax.axis_size("col")
    own_blocks, edge, rank = basis.shape
    blocks_all = block_order.shape[0]
    scale = jnp.sqrt(jnp.float32(blocks_all * edge))
    row_here = lax.axis_index("row")
    row_group = own_blocks * cols_count
    present = tile_list[:, 0] >= 0
    slot_range = jnp.arange(blocks_all, dtype=jnp.int32)
    match = block_order[None, None, :] == tile_list[:, :, None]
    slots_both = jnp.sum(jnp.where(match, slot_range[None, None, :], 0), axis=2)
    first_slot = slots_both[:, 0]
    second_slot = slots_both[:, 1]
    row_local = jnp.where(present, first_slot - row_here * row_group, -1)
    owner_second = second_slot // own_blocks
    col_local = jnp.where(
        present, owner_second // cols_count * own_blocks + second_slot % own_blocks, -1
    )
    column_side = lax.all_gather(basis, "row", axis=0, tiled=True)
    row_side = lax.all_gather(basis, "col", axis=0, tiled=True)
    row_partial, col_partial = tile_products(
        row_local, col_local, tile_values, column_side, row_side
    )
    row_owned = lax.psum_scatter(row_partial, "col", scatter_dimension=0, tiled=True)
    col_owned = lax.psum_scatter(col_partial, "row", scatter_dimension=0, tiled=True)
    product = (row_owned + col_owned).reshape(own_blocks * edge, rank)
    old = basis.reshape(own_blocks * edge, rank).astype(jnp.float32)
    sums = sum_all(jnp.concatenate([gram_of(product, product), gram_of(old, product)], 0), 0)
    gram = sums[:rank]
    projected = sums[rank:] / scale
    first_basis = times_transposed(product, inverse_factor(gram))
    second = sum_all(gram_of(first_basis, first_basis), 1)
    final = times_transposed(first_basis, inverse_factor(second))
    basis_out = (final * scale).astype(jnp.bfloat16).reshape(own_blocks, edge, rank)
    return (basis_out, projected)


def solution(mesh):
    in_specs = (
        P(("row", "col"), None),
        P(("row", "col"), None, None),
        P(),
        P(("row", "col"), None, None),
    )
    out_specs = (P(("row", "col"), None, None), P())
    return jax.shard_map(
        per_device, mesh=mesh, in_specs=in_specs, out_specs=out_specs, check_vma=False
    )
```

```python
import functools

import jax
import jax.numpy as jnp
from jax import lax
from jax.experimental import pallas as pl
from jax.experimental.pallas import tpu as pltpu
from jax.sharding import PartitionSpec as P

MESH = pl.DeviceIdType.MESH
HIGHEST = lax.Precision.HIGHEST
VMEM_MAX = 67043328


def tile_kernel(row_local, col_local, tile_ref, col_side, row_side, row_out, col_out):
    t = pl.program_id(0)

    @pl.when(t == 0)
    def _():
        @pl.loop(0, row_out.shape[0])
        def _(i):
            row_out[i] = jnp.zeros(row_out.shape[1:], jnp.float32)

        @pl.loop(0, col_out.shape[0])
        def _(i):
            col_out[i] = jnp.zeros(col_out.shape[1:], jnp.float32)

    r = row_local[t]
    c = col_local[t]

    @pl.when(r >= 0)
    def _():
        tile = tile_ref[0]
        row_out[r] += jnp.dot(tile, col_side[c], preferred_element_type=jnp.float32)
        col_out[c] += lax.dot_general(
            tile, row_side[r], (((0,), (0,)), ((), ())), preferred_element_type=jnp.float32
        )


def tile_products(row_local, col_local, tiles, col_side, row_side):
    count, edge, _ = tiles.shape
    rank = col_side.shape[2]
    rows, cols = row_side.shape[0], col_side.shape[0]

    def whole(n):
        return pl.BlockSpec(
            (n, edge, rank), lambda t, *_: (0, 0, 0), pipeline_mode=pl.Buffered(1)
        )

    return pl.pallas_call(
        tile_kernel,
        grid_spec=pltpu.PrefetchScalarGridSpec(
            num_scalar_prefetch=2,
            grid=(count,),
            in_specs=[
                pl.BlockSpec((1, edge, edge), lambda t, *_: (t, 0, 0)),
                whole(cols),
                whole(rows),
            ],
            out_specs=[whole(rows), whole(cols)],
        ),
        out_shape=[
            jax.ShapeDtypeStruct((rows, edge, rank), jnp.float32),
            jax.ShapeDtypeStruct((cols, edge, rank), jnp.float32),
        ],
        compiler_params=pltpu.CompilerParams(vmem_limit_bytes=VMEM_MAX),
        name="tile_products",
    )(row_local, col_local, tiles, col_side, row_side)


def sum_kernel(nr, nc, x_ref, out_ref, land_row, mid, land_col, send_sem, recv_sem):
    r = lax.axis_index("row")
    c = lax.axis_index("col")

    def row_peer(o):
        return lax.rem(r + o, nr)

    def col_peer(o):
        return lax.rem(c + o, nc)

    barrier = pltpu.get_barrier_semaphore()
    for o in range(1, nr):
        pl.semaphore_signal(barrier, inc=1, device_id=(row_peer(o), c), device_id_type=MESH)
    for o in range(1, nc):
        pl.semaphore_signal(barrier, inc=1, device_id=(r, col_peer(o)), device_id_type=MESH)
    pl.semaphore_wait(barrier, nr + nc - 2)

    def copy(src, dst, sem, device):
        return pltpu.make_async_remote_copy(
            src_ref=src,
            dst_ref=dst,
            send_sem=send_sem.at[sem],
            recv_sem=recv_sem.at[sem],
            device_id=device,
            device_id_type=MESH,
        )

    base = 0
    copies = []
    for o in range(1, nr):
        p = row_peer(o)
        copies.append(copy(x_ref.at[p], land_row.at[o - 1], base + o - 1, (p, c)))
    for k in copies:
        k.start()
    total = x_ref[r]
    for o, k in enumerate(copies):
        k.wait_recv()
        total += land_row[o]
    mid[...] = total
    sent = copies

    base += nr - 1
    copies = []
    for o in range(1, nc):
        p = col_peer(o)
        copies.append(copy(mid.at[p], land_col.at[o - 1], base + o - 1, (r, p)))
    for k in copies:
        k.start()
    total = mid[c]
    for o, k in enumerate(copies):
        k.wait_recv()
        total += land_col[o]
    out_ref[r, c] = total
    sent = sent + copies

    base += nc - 1
    copies = []
    for o in range(1, nc):
        p = col_peer(o)
        copies.append(copy(out_ref.at[r, c], out_ref.at[r, c], base + o - 1, (r, p)))
    for k in copies:
        k.start()
    for k in copies:
        k.wait_recv()
    sent = sent + copies

    base += nc - 1
    copies = []
    for o in range(1, nr):
        p = row_peer(o)
        copies.append(copy(out_ref.at[r], out_ref.at[r], base + o - 1, (p, c)))
    for k in copies:
        k.start()
    for k in copies:
        k.wait_recv()
    for k in sent + copies:
        k.wait_send()


def sum_all(x, collective_id):
    nr, nc = lax.axis_size("row"), lax.axis_size("col")
    rows, rank = x.shape
    part = rows // (nr * nc)
    sems = 2 * (nr + nc - 2)
    y = pl.pallas_call(
        functools.partial(sum_kernel, nr, nc),
        out_shape=jax.ShapeDtypeStruct((nr, nc, part, rank), jnp.float32),
        in_specs=[pl.BlockSpec(memory_space=pltpu.VMEM)],
        out_specs=pl.BlockSpec(memory_space=pltpu.VMEM),
        scratch_shapes=[
            pltpu.VMEM((nr - 1, nc, part, rank), jnp.float32),
            pltpu.VMEM((nc, part, rank), jnp.float32),
            pltpu.VMEM((nc - 1, part, rank), jnp.float32),
            pltpu.SemaphoreType.DMA((sems,)),
            pltpu.SemaphoreType.DMA((sems,)),
        ],
        compiler_params=pltpu.CompilerParams(collective_id=collective_id, has_side_effects=True),
        name="sum_all",
    )(x.reshape(nr, nc, part, rank))
    return y.reshape(rows, rank)


class Side:
    def __init__(self, axis, count, inner_count):
        self.axis = axis
        self.inner_count = inner_count
        self.outer_count = count // inner_count
        index = lax.axis_index(axis)
        self.inner = lax.rem(index, inner_count)
        self.outer = lax.div(index, inner_count)

    def place(self, outer_step, inner_step):
        outer = lax.rem(self.outer + outer_step, self.outer_count)
        inner = lax.rem(self.inner + inner_step, self.inner_count)
        return outer * self.inner_count + inner

    def device(self, outer_step, inner_step):
        index = self.place(outer_step, inner_step)
        if self.axis == "row":
            return (index, lax.axis_index("col"))
        return (lax.axis_index("row"), index)

    def peers(self):
        inner = [(0, t) for t in range(1, self.inner_count)]
        return inner + [(s, 0) for s in range(1, self.outer_count)]


def inner_of(count):
    inner = 1
    while inner * inner * 4 <= count:
        inner *= 2
    return inner


def make_sides(nr, nc):
    return Side("row", nr, 2), Side("col", nc, inner_of(nc))


def greet(sides):
    barrier = pltpu.get_barrier_semaphore()
    total = 0
    for side in sides:
        for step in side.peers():
            pl.semaphore_signal(
                barrier, inc=1, device_id=side.device(*step), device_id_type=MESH
            )
            total += 1
    pl.semaphore_wait(barrier, total)


class Sender:
    def __init__(self, send_sem, recv_sem):
        self.send_sem, self.recv_sem, self.sent = send_sem, recv_sem, []

    def start(self, src, dst, device):
        n = len(self.sent)
        copy = pltpu.make_async_remote_copy(
            src_ref=src,
            dst_ref=dst,
            send_sem=self.send_sem.at[n],
            recv_sem=self.recv_sem.at[n],
            device_id=device,
            device_id_type=MESH,
        )
        copy.start()
        self.sent.append(copy)
        return copy

    def finish(self):
        for copy in self.sent:
            copy.wait_send()


def gather_kernel(nr, nc, own, own_ref, col_side, row_side, send_sem, recv_sem, local_sem):
    sides = make_sides(nr, nc)
    outs = (col_side, row_side)
    greet(sides)
    sender = Sender(send_sem, recv_sem)

    def at(out, index):
        return out.at[pl.ds(index * own, own)]

    first = []
    for side, out in zip(sides, outs):
        mine = at(out, side.place(0, 0))
        for t in range(1, side.inner_count):
            first.append(sender.start(own_ref, mine, side.device(0, t)))
    outer = []
    for side, out in zip(sides, outs):
        mine = at(out, side.place(0, 0))
        for s in range(1, side.outer_count):
            outer.append((side, out, s, sender.start(own_ref, mine, side.device(s, 0))))
    local = []
    for k, (side, out) in enumerate(zip(sides, outs)):
        copy = pltpu.make_async_copy(own_ref, at(out, side.place(0, 0)), local_sem.at[k])
        copy.start()
        local.append(copy)
    for side, out, s, copy in outer:
        copy.wait_recv()
        got = at(out, side.place(side.outer_count - s, 0))
        for t in range(1, side.inner_count):
            first.append(sender.start(got, got, side.device(0, t)))
    for copy in first:
        copy.wait_recv()
    for copy in local:
        copy.wait()
    sender.finish()


def side_copies(count, inner):
    outer = count // inner
    return outer - 1 + outer * (inner - 1)


def gather_sides(basis):
    nr, nc = lax.axis_size("row"), lax.axis_size("col")
    own = basis.shape[0]
    sems = side_copies(nr, 2) + side_copies(nc, inner_of(nc))
    return pl.pallas_call(
        functools.partial(gather_kernel, nr, nc, own),
        out_shape=[
            jax.ShapeDtypeStruct((n * own,) + basis.shape[1:], basis.dtype) for n in (nr, nc)
        ],
        in_specs=[pl.BlockSpec(memory_space=pltpu.VMEM)],
        out_specs=[pl.BlockSpec(memory_space=pl.ANY)] * 2,
        scratch_shapes=[
            pltpu.SemaphoreType.DMA((sems,)),
            pltpu.SemaphoreType.DMA((sems,)),
            pltpu.SemaphoreType.DMA((2,)),
        ],
        compiler_params=pltpu.CompilerParams(collective_id=2, has_side_effects=True),
        name="gather_sides",
    )(basis)


def add_into(dst, src):
    edge = dst.shape[0]
    step = min(64, edge)

    @pl.loop(0, edge // step)
    def _(i):
        part = pl.ds(pl.multiple_of(i * step, step), step)
        dst[part, :] += src[part, :]


def scatter_kernel(nr, nc, own, col_ref, row_ref, out_ref, *scratch):
    bufs, (send_sem, recv_sem, local_sem) = scratch[:-3], scratch[-3:]
    sides = make_sides(nr, nc)
    greet(sides)
    sender = Sender(send_sem, recv_sem)
    local_count = 0
    plans = []
    for side, ref, k in ((sides[0], col_ref, 0), (sides[1], row_ref, 3)):
        mid, land_in, land_out = bufs[k : k + 3]
        steps = []
        for s in range(1, side.outer_count + 1):
            for b in range(own):
                waits = []
                for t in range(1, side.inner_count):
                    waits.append(
                        sender.start(
                            ref.at[side.place(s, t) * own + b],
                            land_in.at[t - 1, s - 1, b],
                            side.device(0, t),
                        )
                    )
                keep = pltpu.make_async_copy(
                    ref.at[side.place(s, 0) * own + b], mid.at[s - 1, b], local_sem.at[local_count]
                )
                keep.start()
                local_count += 1
                steps.append((s, b, waits, keep))
        plans.append((side, mid, land_in, land_out, steps))
    arrivals = []
    for side, mid, land_in, land_out, steps in plans:
        for s, b, waits, keep in steps:
            keep.wait()
            for t, copy in enumerate(waits):
                copy.wait_recv()
                add_into(mid.at[s - 1, b], land_in.at[t, s - 1, b])
            if s < side.outer_count:
                copy = sender.start(
                    mid.at[s - 1, b], land_out.at[s - 1, b], side.device(s, 0)
                )
                arrivals.append((mid, land_out, s, b, side, copy))
    for mid, land_out, s, b, side, copy in arrivals:
        copy.wait_recv()
        add_into(mid.at[side.outer_count - 1, b], land_out.at[s - 1, b])
    col_mid, row_mid = plans[0][1], plans[1][1]
    col_last, row_last = plans[0][0].outer_count - 1, plans[1][0].outer_count - 1
    edge = out_ref.shape[1]
    step = min(64, edge)
    for b in range(own):

        @pl.loop(0, edge // step)
        def _(i):
            part = pl.ds(pl.multiple_of(i * step, step), step)
            out_ref[b, part, :] = col_mid[col_last, b, part, :] + row_mid[row_last, b, part, :]

    sender.finish()


def scatter_sums(col_partial, row_partial, own):
    nr, nc = lax.axis_size("row"), lax.axis_size("col")
    block = col_partial.shape[1:]
    scratch = []
    for count, inner in ((nr, 2), (nc, inner_of(nc))):
        outer = count // inner
        scratch += [
            pltpu.VMEM((outer, own) + block, jnp.float32),
            pltpu.VMEM((max(inner - 1, 1), outer, own) + block, jnp.float32),
            pltpu.VMEM((max(outer - 1, 1), own) + block, jnp.float32),
        ]
    sems = own * (side_copies(nr, 2) + side_copies(nc, inner_of(nc)))
    locals_ = own * (nr // 2 + nc // inner_of(nc))
    return pl.pallas_call(
        functools.partial(scatter_kernel, nr, nc, own),
        out_shape=jax.ShapeDtypeStruct((own,) + block, jnp.float32),
        in_specs=[pl.BlockSpec(memory_space=pl.ANY)] * 2,
        out_specs=pl.BlockSpec(memory_space=pltpu.VMEM),
        scratch_shapes=scratch
        + [
            pltpu.SemaphoreType.DMA((sems,)),
            pltpu.SemaphoreType.DMA((sems,)),
            pltpu.SemaphoreType.DMA((locals_,)),
        ],
        compiler_params=pltpu.CompilerParams(
            collective_id=3, has_side_effects=True, vmem_limit_bytes=VMEM_MAX
        ),
        name="scatter_sums",
    )(col_partial, row_partial)


def invert_panel(x):
    n = x.shape[0]
    rows = lax.broadcasted_iota(jnp.int32, (n, n), 0)
    cols = lax.broadcasted_iota(jnp.int32, (n, n), 1)
    pivots = jnp.ones((n, n), jnp.float32)
    for j in range(n):
        column = jnp.broadcast_to(x[:, j : j + 1], (n, n))
        pivot = column[j : j + 1, :]
        line = jnp.where(cols[j : j + 1, :] == j, 1.0, x[j : j + 1, :]) / pivot
        pivots = jnp.where(rows == j, column, pivots)
        base = jnp.where(cols == j, 0.0, x)
        x = base - jnp.where(rows > j, column, 0.0) * jnp.broadcast_to(line, (n, n))
        x = jnp.where((cols == j) & (rows == j), 1.0, x)
    x = jnp.where(rows == cols, 1.0, jnp.where(rows > cols, x, 0.0))
    return x * lax.rsqrt(pivots)


def inverse_kernel(panel, a_ref, out_ref):
    rank = a_ref.shape[0]
    out_ref[...] = a_ref[...]
    for k in range(rank // panel):
        lo, hi = k * panel, (k + 1) * panel
        inv = invert_panel(out_ref[lo:hi, lo:hi])
        out_ref[lo:hi, lo:hi] = inv
        strip = out_ref[lo:hi, :]
        cols = lax.broadcasted_iota(jnp.int32, strip.shape, 1)
        new = jnp.dot(inv, strip, precision=HIGHEST, preferred_element_type=jnp.float32)
        done = jnp.where((cols >= lo) & (cols < hi), strip, new)
        out_ref[lo:hi, :] = jnp.where(cols < hi, done, 0.0)
        if hi < rank:
            out_ref[hi:, lo:hi] = jnp.zeros((rank - hi, panel), jnp.float32)
            out_ref[hi:, :] -= lax.dot_general(
                new,
                done,
                (((0,), (0,)), ((), ())),
                precision=HIGHEST,
                preferred_element_type=jnp.float32,
            )[hi:, :]


def inverse_factor(a):
    return pl.pallas_call(
        functools.partial(inverse_kernel, 32),
        out_shape=jax.ShapeDtypeStruct(a.shape, jnp.float32),
        in_specs=[pl.BlockSpec(memory_space=pltpu.VMEM)],
        out_specs=pl.BlockSpec(memory_space=pltpu.VMEM),
        name="inverse_factor",
    )(a)


def times_transposed(x, m):
    return lax.dot_general(x, m, (((1,), (1,)), ((), ())), precision=HIGHEST)


def gram_of(x, y):
    return lax.dot_general(x, y, (((0,), (0,)), ((), ())), precision=HIGHEST)


def per_device(tile_list, tile_values, block_order, basis):
    rows_count = lax.axis_size("row")
    cols_count = lax.axis_size("col")
    own_blocks, edge, rank = basis.shape
    blocks_all = block_order.shape[0]
    scale = jnp.sqrt(jnp.float32(blocks_all * edge))
    row_here = lax.axis_index("row")
    row_group = own_blocks * cols_count
    present = tile_list[:, 0] >= 0
    slot_range = jnp.arange(blocks_all, dtype=jnp.int32)
    match = block_order[None, None, :] == tile_list[:, :, None]
    slots_both = jnp.sum(jnp.where(match, slot_range[None, None, :], 0), axis=2)
    first_slot = slots_both[:, 0]
    second_slot = slots_both[:, 1]
    row_local = jnp.where(present, first_slot - row_here * row_group, -1)
    owner_second = second_slot // own_blocks
    col_local = jnp.where(
        present, owner_second // cols_count * own_blocks + second_slot % own_blocks, -1
    )
    column_side, row_side = gather_sides(basis)
    row_partial, col_partial = tile_products(
        row_local, col_local, tile_values, column_side, row_side
    )
    product = scatter_sums(col_partial, row_partial, own_blocks).reshape(own_blocks * edge, rank)
    old = basis.reshape(own_blocks * edge, rank).astype(jnp.float32)
    sums = sum_all(jnp.concatenate([gram_of(product, product), gram_of(old, product)], 0), 0)
    gram = sums[:rank]
    projected = sums[rank:] / scale
    first_basis = times_transposed(product, inverse_factor(gram))
    second = sum_all(gram_of(first_basis, first_basis), 1)
    final = times_transposed(first_basis, inverse_factor(second))
    basis_out = (final * scale).astype(jnp.bfloat16).reshape(own_blocks, edge, rank)
    return (basis_out, projected)


def solution(mesh):
    in_specs = (
        P(("row", "col"), None),
        P(("row", "col"), None, None),
        P(),
        P(("row", "col"), None, None),
    )
    out_specs = (P(("row", "col"), None, None), P())
    return jax.shard_map(
        per_device, mesh=mesh, in_specs=in_specs, out_specs=out_specs, check_vma=False
    )
```

```python
import functools

import jax
import jax.numpy as jnp
from jax import lax
from jax.experimental import pallas as pl
from jax.experimental.pallas import tpu as pltpu
from jax.sharding import PartitionSpec as P

MESH = pl.DeviceIdType.MESH
HIGHEST = lax.Precision.HIGHEST
VMEM_MAX = 67043328


def tile_kernel(row_local, col_local, tile_ref, col_side, row_side, row_out, col_out):
    t = pl.program_id(0)

    @pl.when(t == 0)
    def _():
        @pl.loop(0, row_out.shape[0])
        def _(i):
            row_out[i] = jnp.zeros(row_out.shape[1:], jnp.float32)

        @pl.loop(0, col_out.shape[0])
        def _(i):
            col_out[i] = jnp.zeros(col_out.shape[1:], jnp.float32)

    r = row_local[t]
    c = col_local[t]

    @pl.when(r >= 0)
    def _():
        tile = tile_ref[0]
        row_out[r] += jnp.dot(tile, col_side[c], preferred_element_type=jnp.float32)
        col_out[c] += lax.dot_general(
            tile, row_side[r], (((0,), (0,)), ((), ())), preferred_element_type=jnp.float32
        )


def tile_products(row_local, col_local, tiles, col_side, row_side):
    count, edge, _ = tiles.shape
    rank = col_side.shape[2]
    rows, cols = row_side.shape[0], col_side.shape[0]

    def whole(n):
        return pl.BlockSpec(
            (n, edge, rank), lambda t, *_: (0, 0, 0), pipeline_mode=pl.Buffered(1)
        )

    return pl.pallas_call(
        tile_kernel,
        grid_spec=pltpu.PrefetchScalarGridSpec(
            num_scalar_prefetch=2,
            grid=(count,),
            in_specs=[
                pl.BlockSpec((1, edge, edge), lambda t, *_: (t, 0, 0)),
                whole(cols),
                whole(rows),
            ],
            out_specs=[whole(rows), whole(cols)],
        ),
        out_shape=[
            jax.ShapeDtypeStruct((rows, edge, rank), jnp.float32),
            jax.ShapeDtypeStruct((cols, edge, rank), jnp.float32),
        ],
        compiler_params=pltpu.CompilerParams(vmem_limit_bytes=VMEM_MAX),
        name="tile_products",
    )(row_local, col_local, tiles, col_side, row_side)


def sum_kernel(nr, nc, x_ref, out_ref, land_row, mid, land_col, send_sem, recv_sem):
    r = lax.axis_index("row")
    c = lax.axis_index("col")

    def row_peer(o):
        return lax.rem(r + o, nr)

    def col_peer(o):
        return lax.rem(c + o, nc)

    barrier = pltpu.get_barrier_semaphore()
    for o in range(1, nr):
        pl.semaphore_signal(barrier, inc=1, device_id=(row_peer(o), c), device_id_type=MESH)
    for o in range(1, nc):
        pl.semaphore_signal(barrier, inc=1, device_id=(r, col_peer(o)), device_id_type=MESH)
    pl.semaphore_wait(barrier, nr + nc - 2)

    def copy(src, dst, sem, device):
        return pltpu.make_async_remote_copy(
            src_ref=src,
            dst_ref=dst,
            send_sem=send_sem.at[sem],
            recv_sem=recv_sem.at[sem],
            device_id=device,
            device_id_type=MESH,
        )

    base = 0
    copies = []
    for o in range(1, nr):
        p = row_peer(o)
        copies.append(copy(x_ref.at[p], land_row.at[o - 1], base + o - 1, (p, c)))
    for k in copies:
        k.start()
    total = x_ref[r]
    for o, k in enumerate(copies):
        k.wait_recv()
        total += land_row[o]
    mid[...] = total
    sent = copies

    base += nr - 1
    copies = []
    for o in range(1, nc):
        p = col_peer(o)
        copies.append(copy(mid.at[p], land_col.at[o - 1], base + o - 1, (r, p)))
    for k in copies:
        k.start()
    total = mid[c]
    for o, k in enumerate(copies):
        k.wait_recv()
        total += land_col[o]
    out_ref[r, c] = total
    sent = sent + copies

    base += nc - 1
    copies = []
    for o in range(1, nc):
        p = col_peer(o)
        copies.append(copy(out_ref.at[r, c], out_ref.at[r, c], base + o - 1, (r, p)))
    for k in copies:
        k.start()
    for k in copies:
        k.wait_recv()
    sent = sent + copies

    base += nc - 1
    copies = []
    for o in range(1, nr):
        p = row_peer(o)
        copies.append(copy(out_ref.at[r], out_ref.at[r], base + o - 1, (p, c)))
    for k in copies:
        k.start()
    for k in copies:
        k.wait_recv()
    for k in sent + copies:
        k.wait_send()


def sum_all(x, collective_id):
    nr, nc = lax.axis_size("row"), lax.axis_size("col")
    rows, rank = x.shape
    part = rows // (nr * nc)
    sems = 2 * (nr + nc - 2)
    y = pl.pallas_call(
        functools.partial(sum_kernel, nr, nc),
        out_shape=jax.ShapeDtypeStruct((nr, nc, part, rank), jnp.float32),
        in_specs=[pl.BlockSpec(memory_space=pltpu.VMEM)],
        out_specs=pl.BlockSpec(memory_space=pltpu.VMEM),
        scratch_shapes=[
            pltpu.VMEM((nr - 1, nc, part, rank), jnp.float32),
            pltpu.VMEM((nc, part, rank), jnp.float32),
            pltpu.VMEM((nc - 1, part, rank), jnp.float32),
            pltpu.SemaphoreType.DMA((sems,)),
            pltpu.SemaphoreType.DMA((sems,)),
        ],
        compiler_params=pltpu.CompilerParams(collective_id=collective_id, has_side_effects=True),
        name="sum_all",
    )(x.reshape(nr, nc, part, rank))
    return y.reshape(rows, rank)


class Side:
    def __init__(self, axis, count, inner_count):
        self.axis = axis
        self.inner_count = inner_count
        self.outer_count = count // inner_count
        index = lax.axis_index(axis)
        self.inner = lax.rem(index, inner_count)
        self.outer = lax.div(index, inner_count)

    def place(self, outer_step, inner_step):
        outer = lax.rem(self.outer + outer_step, self.outer_count)
        inner = lax.rem(self.inner + inner_step, self.inner_count)
        return outer * self.inner_count + inner

    def device(self, outer_step, inner_step):
        index = self.place(outer_step, inner_step)
        if self.axis == "row":
            return (index, lax.axis_index("col"))
        return (lax.axis_index("row"), index)

    def peers(self):
        inner = [(0, t) for t in range(1, self.inner_count)]
        return inner + [(s, 0) for s in range(1, self.outer_count)]


def inner_of(count):
    inner = 1
    while inner * inner * 4 <= count:
        inner *= 2
    return inner


def make_sides(nr, nc):
    return Side("row", nr, 2), Side("col", nc, inner_of(nc))


def greet(sides):
    barrier = pltpu.get_barrier_semaphore()
    total = 0
    for side in sides:
        for step in side.peers():
            pl.semaphore_signal(
                barrier, inc=1, device_id=side.device(*step), device_id_type=MESH
            )
            total += 1
    pl.semaphore_wait(barrier, total)


class Sender:
    def __init__(self, send_sem, recv_sem):
        self.send_sem, self.recv_sem, self.sent = send_sem, recv_sem, []

    def start(self, src, dst, device):
        n = len(self.sent)
        copy = pltpu.make_async_remote_copy(
            src_ref=src,
            dst_ref=dst,
            send_sem=self.send_sem.at[n],
            recv_sem=self.recv_sem.at[n],
            device_id=device,
            device_id_type=MESH,
        )
        copy.start()
        self.sent.append(copy)
        return copy

    def finish(self):
        for copy in self.sent:
            copy.wait_send()


def gather_kernel(nr, nc, own, own_ref, col_side, row_side, send_sem, recv_sem, local_sem):
    sides = make_sides(nr, nc)
    outs = (col_side, row_side)
    greet(sides)
    sender = Sender(send_sem, recv_sem)
    first, outer, local = [], [], []
    for k, (side, out) in reversed(list(enumerate(zip(sides, outs)))):
        mine = side.place(0, 0) * own
        for s in range(1, side.outer_count):
            for b in range(own):
                copy = sender.start(own_ref.at[b], out.at[mine + b], side.device(s, 0))
                outer.append((side, out, s, b, copy))
        for t in range(1, side.inner_count):
            for b in range(own):
                first.append(
                    sender.start(own_ref.at[b], out.at[mine + b], side.device(0, t))
                )
        copy = pltpu.make_async_copy(own_ref, out.at[pl.ds(mine, own)], local_sem.at[k])
        copy.start()
        local.append(copy)
    for side, out, s, b, copy in outer:
        copy.wait_recv()
        got = out.at[side.place(side.outer_count - s, 0) * own + b]
        for t in range(1, side.inner_count):
            first.append(sender.start(got, got, side.device(0, t)))
    for copy in first:
        copy.wait_recv()
    for copy in local:
        copy.wait()
    sender.finish()


def side_copies(count, inner):
    outer = count // inner
    return outer - 1 + outer * (inner - 1)


def gather_sides(basis):
    nr, nc = lax.axis_size("row"), lax.axis_size("col")
    own = basis.shape[0]
    sems = own * (side_copies(nr, 2) + side_copies(nc, inner_of(nc)))
    return pl.pallas_call(
        functools.partial(gather_kernel, nr, nc, own),
        out_shape=[
            jax.ShapeDtypeStruct((n * own,) + basis.shape[1:], basis.dtype) for n in (nr, nc)
        ],
        in_specs=[pl.BlockSpec(memory_space=pltpu.VMEM)],
        out_specs=[pl.BlockSpec(memory_space=pl.ANY)] * 2,
        scratch_shapes=[
            pltpu.SemaphoreType.DMA((sems,)),
            pltpu.SemaphoreType.DMA((sems,)),
            pltpu.SemaphoreType.DMA((2,)),
        ],
        compiler_params=pltpu.CompilerParams(collective_id=2, has_side_effects=True),
        name="gather_sides",
    )(basis)


def add_into(dst, src):
    edge = dst.shape[0]
    step = min(64, edge)

    @pl.loop(0, edge // step)
    def _(i):
        part = pl.ds(pl.multiple_of(i * step, step), step)
        dst[part, :] += src[part, :]


def scatter_kernel(nr, nc, own, col_ref, row_ref, out_ref, *scratch):
    bufs, (send_sem, recv_sem, local_sem) = scratch[:-3], scratch[-3:]
    sides = make_sides(nr, nc)
    greet(sides)
    sender = Sender(send_sem, recv_sem)
    local_count = 0
    plans = []
    for side, ref, k in ((sides[0], col_ref, 0), (sides[1], row_ref, 3)):
        mid, land_in, land_out = bufs[k : k + 3]
        steps = []
        middle = side.outer_count // 2
        for s in sorted(range(1, side.outer_count + 1), key=lambda s: (s != middle, s)):
            for b in range(own):
                waits = []
                for t in range(1, side.inner_count):
                    waits.append(
                        sender.start(
                            ref.at[side.place(s, t) * own + b],
                            land_in.at[t - 1, s - 1, b],
                            side.device(0, t),
                        )
                    )
                keep = pltpu.make_async_copy(
                    ref.at[side.place(s, 0) * own + b], mid.at[s - 1, b], local_sem.at[local_count]
                )
                keep.start()
                local_count += 1
                steps.append((s, b, waits, keep))
        plans.append((side, mid, land_in, land_out, steps))
    arrivals = []
    for side, mid, land_in, land_out, steps in plans:
        for s, b, waits, keep in steps:
            keep.wait()
            for t, copy in enumerate(waits):
                copy.wait_recv()
                add_into(mid.at[s - 1, b], land_in.at[t, s - 1, b])
            if s < side.outer_count:
                copy = sender.start(
                    mid.at[s - 1, b], land_out.at[s - 1, b], side.device(s, 0)
                )
                arrivals.append((mid, land_out, s, b, side, copy))
    for mid, land_out, s, b, side, copy in arrivals:
        copy.wait_recv()
        add_into(mid.at[side.outer_count - 1, b], land_out.at[s - 1, b])
    col_mid, row_mid = plans[0][1], plans[1][1]
    col_last, row_last = plans[0][0].outer_count - 1, plans[1][0].outer_count - 1
    edge = out_ref.shape[1]
    step = min(64, edge)
    for b in range(own):

        @pl.loop(0, edge // step)
        def _(i):
            part = pl.ds(pl.multiple_of(i * step, step), step)
            out_ref[b, part, :] = col_mid[col_last, b, part, :] + row_mid[row_last, b, part, :]

    sender.finish()


def scatter_sums(col_partial, row_partial, own):
    nr, nc = lax.axis_size("row"), lax.axis_size("col")
    block = col_partial.shape[1:]
    scratch = []
    for count, inner in ((nr, 2), (nc, inner_of(nc))):
        outer = count // inner
        scratch += [
            pltpu.VMEM((outer, own) + block, jnp.float32),
            pltpu.VMEM((max(inner - 1, 1), outer, own) + block, jnp.float32),
            pltpu.VMEM((max(outer - 1, 1), own) + block, jnp.float32),
        ]
    sems = own * (side_copies(nr, 2) + side_copies(nc, inner_of(nc)))
    locals_ = own * (nr // 2 + nc // inner_of(nc))
    return pl.pallas_call(
        functools.partial(scatter_kernel, nr, nc, own),
        out_shape=jax.ShapeDtypeStruct((own,) + block, jnp.float32),
        in_specs=[pl.BlockSpec(memory_space=pl.ANY)] * 2,
        out_specs=pl.BlockSpec(memory_space=pltpu.VMEM),
        scratch_shapes=scratch
        + [
            pltpu.SemaphoreType.DMA((sems,)),
            pltpu.SemaphoreType.DMA((sems,)),
            pltpu.SemaphoreType.DMA((locals_,)),
        ],
        compiler_params=pltpu.CompilerParams(
            collective_id=3, has_side_effects=True, vmem_limit_bytes=VMEM_MAX
        ),
        name="scatter_sums",
    )(col_partial, row_partial)


def invert_panel(x):
    n = x.shape[0]
    rows = lax.broadcasted_iota(jnp.int32, (n, n), 0)
    cols = lax.broadcasted_iota(jnp.int32, (n, n), 1)
    pivots = jnp.ones((n, n), jnp.float32)
    group = 4
    for start in range(0, n, group):
        members = range(start, start + group)
        columns = {j: jnp.broadcast_to(x[:, j : j + 1], (n, n)) for j in members}
        for j in members:
            column = columns[j]
            pivot = column[j : j + 1, :]
            inverse = 1.0 / pivot
            below = jnp.where(rows > j, column, 0.0)
            for k in range(j + 1, start + group):
                factor = columns[k][j : j + 1, :] * inverse
                columns[k] = columns[k] - below * jnp.broadcast_to(factor, (n, n))
            line = jnp.where(cols[j : j + 1, :] == j, 1.0, x[j : j + 1, :]) * inverse
            pivots = jnp.where(rows == j, column, pivots)
            base = jnp.where(cols == j, jnp.where(rows == j, 1.0, 0.0), x)
            x = base - below * jnp.broadcast_to(line, (n, n))
    x = jnp.where(rows == cols, 1.0, jnp.where(rows > cols, x, 0.0))
    return x * lax.rsqrt(pivots)


def eliminate(panel, a_ref, out_ref):
    rank = a_ref.shape[0]
    out_ref[...] = a_ref[...]
    for k in range(rank // panel):
        lo, hi = k * panel, (k + 1) * panel
        inv = invert_panel(out_ref[lo:hi, lo:hi])
        out_ref[lo:hi, lo:hi] = inv
        strip = out_ref[lo:hi, :]
        cols = lax.broadcasted_iota(jnp.int32, strip.shape, 1)
        new = jnp.dot(inv, strip, precision=HIGHEST, preferred_element_type=jnp.float32)
        done = jnp.where((cols >= lo) & (cols < hi), strip, new)
        out_ref[lo:hi, :] = jnp.where(cols < hi, done, 0.0)
        if hi < rank:
            out_ref[hi:, lo:hi] = jnp.zeros((rank - hi, panel), jnp.float32)
            out_ref[hi:, :] -= lax.dot_general(
                new,
                done,
                (((0,), (0,)), ((), ())),
                precision=HIGHEST,
                preferred_element_type=jnp.float32,
            )[hi:, :]


def inverse_kernel(panel, near_identity, a_ref, out_ref):
    if not near_identity:
        eliminate(panel, a_ref, out_ref)
        return
    rows = lax.broadcasted_iota(jnp.int32, a_ref.shape, 0)
    cols = lax.broadcasted_iota(jnp.int32, a_ref.shape, 1)
    unit = jnp.where(rows == cols, 1.0, 0.0)

    def lower_half(e):
        return jnp.where(rows > cols, e, jnp.where(rows == cols, 0.5 * e, 0.0))

    def dot(x, y, contract):
        return lax.dot_general(
            x,
            y,
            (((1,), (contract,)), ((), ())),
            precision=HIGHEST,
            preferred_element_type=jnp.float32,
        )

    error = a_ref[...] - unit
    size = jnp.sum(error * error)
    near = size < 0.04

    @pl.when(jnp.logical_not(near))
    def _():
        eliminate(panel, a_ref, out_ref)

    @pl.when(near)
    def _():
        out_ref[...] = unit - lower_half(error)

        def more(carry):
            step, last = carry
            return (step < 4) & (last > 1e-9)

        def improve(carry):
            step, _ = carry
            w = out_ref[...]
            e = dot(dot(w, a_ref[...], 0), w, 1) - unit
            out_ref[...] = w - dot(lower_half(e), w, 0)
            return step + 1, jnp.sum(e * e)

        lax.while_loop(more, improve, (0, size))


def inverse_factor(a, near_identity=False):
    return pl.pallas_call(
        functools.partial(inverse_kernel, 32, near_identity),
        out_shape=jax.ShapeDtypeStruct(a.shape, jnp.float32),
        in_specs=[pl.BlockSpec(memory_space=pltpu.VMEM)],
        out_specs=pl.BlockSpec(memory_space=pltpu.VMEM),
        name="inverse_factor",
    )(a)


def times_transposed(x, m):
    return lax.dot_general(x, m, (((1,), (1,)), ((), ())), precision=HIGHEST)


def gram_of(x, y):
    return lax.dot_general(x, y, (((0,), (0,)), ((), ())), precision=HIGHEST)


def per_device(tile_list, tile_values, block_order, basis):
    rows_count = lax.axis_size("row")
    cols_count = lax.axis_size("col")
    own_blocks, edge, rank = basis.shape
    blocks_all = block_order.shape[0]
    scale = jnp.sqrt(jnp.float32(blocks_all * edge))
    row_here = lax.axis_index("row")
    row_group = own_blocks * cols_count
    present = tile_list[:, 0] >= 0
    slot_range = jnp.arange(blocks_all, dtype=jnp.int32)
    match = block_order[None, None, :] == tile_list[:, :, None]
    slots_both = jnp.sum(jnp.where(match, slot_range[None, None, :], 0), axis=2)
    first_slot = slots_both[:, 0]
    second_slot = slots_both[:, 1]
    row_local = jnp.where(present, first_slot - row_here * row_group, -1)
    owner_second = second_slot // own_blocks
    col_local = jnp.where(
        present, owner_second // cols_count * own_blocks + second_slot % own_blocks, -1
    )
    column_side, row_side = gather_sides(basis)
    row_partial, col_partial = tile_products(
        row_local, col_local, tile_values, column_side, row_side
    )
    product = scatter_sums(col_partial, row_partial, own_blocks).reshape(own_blocks * edge, rank)
    old = basis.reshape(own_blocks * edge, rank).astype(jnp.float32)
    sums = sum_all(jnp.concatenate([gram_of(product, product), gram_of(old, product)], 0), 0)
    gram = sums[:rank]
    projected = sums[rank:] / scale
    first_basis = times_transposed(product, inverse_factor(gram))
    second = sum_all(gram_of(first_basis, first_basis), 1)
    final = times_transposed(first_basis, inverse_factor(second, near_identity=True))
    basis_out = (final * scale).astype(jnp.bfloat16).reshape(own_blocks, edge, rank)
    return (basis_out, projected)


def solution(mesh):
    in_specs = (
        P(("row", "col"), None),
        P(("row", "col"), None, None),
        P(),
        P(("row", "col"), None, None),
    )
    out_specs = (P(("row", "col"), None, None), P())
    return jax.shard_map(
        per_device, mesh=mesh, in_specs=in_specs, out_specs=out_specs, check_vma=False
    )
```

```python
import functools

import jax
import jax.numpy as jnp
from jax import lax
from jax.experimental import pallas as pl
from jax.experimental.pallas import tpu as pltpu
from jax.sharding import PartitionSpec as P

MESH = pl.DeviceIdType.MESH
HIGHEST = lax.Precision.HIGHEST
VMEM_MAX = 67043328


def tile_kernel(row_local, col_local, tile_ref, col_side, row_side, row_out, col_out):
    t = pl.program_id(0)

    @pl.when(t == 0)
    def _():
        @pl.loop(0, row_out.shape[0])
        def _(i):
            row_out[i] = jnp.zeros(row_out.shape[1:], jnp.float32)

        @pl.loop(0, col_out.shape[0])
        def _(i):
            col_out[i] = jnp.zeros(col_out.shape[1:], jnp.float32)

    r = row_local[t]
    c = col_local[t]

    @pl.when(r >= 0)
    def _():
        tile = tile_ref[0]
        row_out[r] += jnp.dot(tile, col_side[c], preferred_element_type=jnp.float32)
        col_out[c] += lax.dot_general(
            tile, row_side[r], (((0,), (0,)), ((), ())), preferred_element_type=jnp.float32
        )


def tile_products(row_local, col_local, tiles, col_side, row_side):
    count, edge, _ = tiles.shape
    rank = col_side.shape[2]
    rows, cols = row_side.shape[0], col_side.shape[0]

    def whole(n):
        return pl.BlockSpec(
            (n, edge, rank), lambda t, *_: (0, 0, 0), pipeline_mode=pl.Buffered(1)
        )

    return pl.pallas_call(
        tile_kernel,
        grid_spec=pltpu.PrefetchScalarGridSpec(
            num_scalar_prefetch=2,
            grid=(count,),
            in_specs=[
                pl.BlockSpec((1, edge, edge), lambda t, *_: (t, 0, 0)),
                whole(cols),
                whole(rows),
            ],
            out_specs=[whole(rows), whole(cols)],
        ),
        out_shape=[
            jax.ShapeDtypeStruct((rows, edge, rank), jnp.float32),
            jax.ShapeDtypeStruct((cols, edge, rank), jnp.float32),
        ],
        compiler_params=pltpu.CompilerParams(vmem_limit_bytes=VMEM_MAX),
        name="tile_products",
    )(row_local, col_local, tiles, col_side, row_side)


def sum_kernel(nr, nc, x_ref, out_ref, land_row, mid, land_col, send_sem, recv_sem):
    r = lax.axis_index("row")
    c = lax.axis_index("col")

    def row_peer(o):
        return lax.rem(r + o, nr)

    def col_peer(o):
        return lax.rem(c + o, nc)

    barrier = pltpu.get_barrier_semaphore()
    for o in range(1, nr):
        pl.semaphore_signal(barrier, inc=1, device_id=(row_peer(o), c), device_id_type=MESH)
    for o in range(1, nc):
        pl.semaphore_signal(barrier, inc=1, device_id=(r, col_peer(o)), device_id_type=MESH)
    pl.semaphore_wait(barrier, nr + nc - 2)

    def copy(src, dst, sem, device):
        return pltpu.make_async_remote_copy(
            src_ref=src,
            dst_ref=dst,
            send_sem=send_sem.at[sem],
            recv_sem=recv_sem.at[sem],
            device_id=device,
            device_id_type=MESH,
        )

    base = 0
    copies = []
    for o in range(1, nr):
        p = row_peer(o)
        copies.append(copy(x_ref.at[p], land_row.at[o - 1], base + o - 1, (p, c)))
    for k in copies:
        k.start()
    total = x_ref[r]
    for o, k in enumerate(copies):
        k.wait_recv()
        total += land_row[o]
    mid[...] = total
    sent = copies

    base += nr - 1
    copies = []
    for o in range(1, nc):
        p = col_peer(o)
        copies.append(copy(mid.at[p], land_col.at[o - 1], base + o - 1, (r, p)))
    for k in copies:
        k.start()
    total = mid[c]
    for o, k in enumerate(copies):
        k.wait_recv()
        total += land_col[o]
    out_ref[r, c] = total
    sent = sent + copies

    base += nc - 1
    copies = []
    for o in range(1, nc):
        p = col_peer(o)
        copies.append(copy(out_ref.at[r, c], out_ref.at[r, c], base + o - 1, (r, p)))
    for k in copies:
        k.start()
    for k in copies:
        k.wait_recv()
    sent = sent + copies

    base += nc - 1
    copies = []
    for o in range(1, nr):
        p = row_peer(o)
        copies.append(copy(out_ref.at[r], out_ref.at[r], base + o - 1, (p, c)))
    for k in copies:
        k.start()
    for k in copies:
        k.wait_recv()
    for k in sent + copies:
        k.wait_send()


def sum_all(x, collective_id):
    nr, nc = lax.axis_size("row"), lax.axis_size("col")
    rows, rank = x.shape
    part = rows // (nr * nc)
    sems = 2 * (nr + nc - 2)
    y = pl.pallas_call(
        functools.partial(sum_kernel, nr, nc),
        out_shape=jax.ShapeDtypeStruct((nr, nc, part, rank), jnp.float32),
        in_specs=[pl.BlockSpec(memory_space=pltpu.VMEM)],
        out_specs=pl.BlockSpec(memory_space=pltpu.VMEM),
        scratch_shapes=[
            pltpu.VMEM((nr - 1, nc, part, rank), jnp.float32),
            pltpu.VMEM((nc, part, rank), jnp.float32),
            pltpu.VMEM((nc - 1, part, rank), jnp.float32),
            pltpu.SemaphoreType.DMA((sems,)),
            pltpu.SemaphoreType.DMA((sems,)),
        ],
        compiler_params=pltpu.CompilerParams(collective_id=collective_id, has_side_effects=True),
        name="sum_all",
    )(x.reshape(nr, nc, part, rank))
    return y.reshape(rows, rank)


class Side:
    def __init__(self, axis, count, inner_count):
        self.axis = axis
        self.inner_count = inner_count
        self.outer_count = count // inner_count
        index = lax.axis_index(axis)
        self.inner = lax.rem(index, inner_count)
        self.outer = lax.div(index, inner_count)

    def place(self, outer_step, inner_step):
        outer = lax.rem(self.outer + outer_step, self.outer_count)
        inner = lax.rem(self.inner + inner_step, self.inner_count)
        return outer * self.inner_count + inner

    def device(self, outer_step, inner_step):
        index = self.place(outer_step, inner_step)
        if self.axis == "row":
            return (index, lax.axis_index("col"))
        return (lax.axis_index("row"), index)

    def peers(self):
        inner = [(0, t) for t in range(1, self.inner_count)]
        return inner + [(s, 0) for s in range(1, self.outer_count)]


def inner_of(count):
    inner = 1
    while inner * inner * 4 <= count:
        inner *= 2
    return inner


def make_sides(nr, nc):
    return Side("row", nr, 2), Side("col", nc, inner_of(nc))


def greet(sides):
    barrier = pltpu.get_barrier_semaphore()
    total = 0
    for side in sides:
        for step in side.peers():
            pl.semaphore_signal(
                barrier, inc=1, device_id=side.device(*step), device_id_type=MESH
            )
            total += 1
    pl.semaphore_wait(barrier, total)


class Sender:
    def __init__(self, send_sem, recv_sem):
        self.send_sem, self.recv_sem, self.sent = send_sem, recv_sem, []

    def start(self, src, dst, device):
        n = len(self.sent)
        copy = pltpu.make_async_remote_copy(
            src_ref=src,
            dst_ref=dst,
            send_sem=self.send_sem.at[n],
            recv_sem=self.recv_sem.at[n],
            device_id=device,
            device_id_type=MESH,
        )
        copy.start()
        self.sent.append(copy)
        return copy

    def finish(self):
        for copy in self.sent:
            copy.wait_send()


def gather_kernel(nr, nc, own, own_ref, col_side, row_side, send_sem, recv_sem, local_sem):
    sides = make_sides(nr, nc)
    outs = (col_side, row_side)
    greet(sides)
    sender = Sender(send_sem, recv_sem)
    first, outer, local = [], [], []
    for k, (side, out) in reversed(list(enumerate(zip(sides, outs)))):
        mine = side.place(0, 0) * own
        for s in range(1, side.outer_count):
            for b in range(own):
                copy = sender.start(own_ref.at[b], out.at[mine + b], side.device(s, 0))
                outer.append((side, out, s, b, copy))
        for t in range(1, side.inner_count):
            for b in range(own):
                first.append(
                    sender.start(own_ref.at[b], out.at[mine + b], side.device(0, t))
                )
        copy = pltpu.make_async_copy(own_ref, out.at[pl.ds(mine, own)], local_sem.at[k])
        copy.start()
        local.append(copy)
    for side, out, s, b, copy in outer:
        copy.wait_recv()
        got = out.at[side.place(side.outer_count - s, 0) * own + b]
        for t in range(1, side.inner_count):
            first.append(sender.start(got, got, side.device(0, t)))
    for copy in first:
        copy.wait_recv()
    for copy in local:
        copy.wait()
    sender.finish()


def side_copies(count, inner):
    outer = count // inner
    return outer - 1 + outer * (inner - 1)


def gather_sides(basis):
    nr, nc = lax.axis_size("row"), lax.axis_size("col")
    own = basis.shape[0]
    sems = own * (side_copies(nr, 2) + side_copies(nc, inner_of(nc)))
    return pl.pallas_call(
        functools.partial(gather_kernel, nr, nc, own),
        out_shape=[
            jax.ShapeDtypeStruct((n * own,) + basis.shape[1:], basis.dtype) for n in (nr, nc)
        ],
        in_specs=[pl.BlockSpec(memory_space=pltpu.VMEM)],
        out_specs=[pl.BlockSpec(memory_space=pl.ANY)] * 2,
        scratch_shapes=[
            pltpu.SemaphoreType.DMA((sems,)),
            pltpu.SemaphoreType.DMA((sems,)),
            pltpu.SemaphoreType.DMA((2,)),
        ],
        compiler_params=pltpu.CompilerParams(collective_id=2, has_side_effects=True),
        name="gather_sides",
    )(basis)


def add_into(dst, src):
    edge = dst.shape[0]
    step = min(64, edge)

    @pl.loop(0, edge // step)
    def _(i):
        part = pl.ds(pl.multiple_of(i * step, step), step)
        dst[part, :] += src[part, :]


def scatter_kernel(nr, nc, own, col_ref, row_ref, out_ref, *scratch):
    bufs, (send_sem, recv_sem, local_sem) = scratch[:-3], scratch[-3:]
    sides = make_sides(nr, nc)
    greet(sides)
    sender = Sender(send_sem, recv_sem)
    local_count = 0
    plans = []
    for side, ref, k in ((sides[0], col_ref, 0), (sides[1], row_ref, 3)):
        mid, land_in, land_out = bufs[k : k + 3]
        steps = []
        middle = side.outer_count // 2
        for s in sorted(range(1, side.outer_count + 1), key=lambda s: (s != middle, s)):
            for b in range(own):
                waits = []
                for t in range(1, side.inner_count):
                    waits.append(
                        sender.start(
                            ref.at[side.place(s, t) * own + b],
                            land_in.at[t - 1, s - 1, b],
                            side.device(0, t),
                        )
                    )
                keep = pltpu.make_async_copy(
                    ref.at[side.place(s, 0) * own + b], mid.at[s - 1, b], local_sem.at[local_count]
                )
                keep.start()
                local_count += 1
                steps.append((s, b, waits, keep))
        plans.append((side, mid, land_in, land_out, steps))
    arrivals = []
    for side, mid, land_in, land_out, steps in plans:
        for s, b, waits, keep in steps:
            keep.wait()
            for t, copy in enumerate(waits):
                copy.wait_recv()
                add_into(mid.at[s - 1, b], land_in.at[t, s - 1, b])
            if s < side.outer_count:
                copy = sender.start(
                    mid.at[s - 1, b], land_out.at[s - 1, b], side.device(s, 0)
                )
                arrivals.append((land_out, (s, b), copy))
    for _, _, copy in arrivals:
        copy.wait_recv()
    edge = out_ref.shape[1]
    step = min(64, edge)
    for b in range(own):
        terms = [mid.at[side.outer_count - 1, b] for side, mid, _, _, _ in plans]
        terms += [land_out.at[s - 1, b] for land_out, (s, block), _ in arrivals if block == b]

        @pl.loop(0, edge // step)
        def _(i):
            part = pl.ds(pl.multiple_of(i * step, step), step)
            total = terms[0][part, :]
            for term in terms[1:]:
                total += term[part, :]
            out_ref[b, part, :] = total

    sender.finish()


def scatter_sums(col_partial, row_partial, own):
    nr, nc = lax.axis_size("row"), lax.axis_size("col")
    block = col_partial.shape[1:]
    scratch = []
    for count, inner in ((nr, 2), (nc, inner_of(nc))):
        outer = count // inner
        scratch += [
            pltpu.VMEM((outer, own) + block, jnp.float32),
            pltpu.VMEM((max(inner - 1, 1), outer, own) + block, jnp.float32),
            pltpu.VMEM((max(outer - 1, 1), own) + block, jnp.float32),
        ]
    sems = own * (side_copies(nr, 2) + side_copies(nc, inner_of(nc)))
    locals_ = own * (nr // 2 + nc // inner_of(nc))
    return pl.pallas_call(
        functools.partial(scatter_kernel, nr, nc, own),
        out_shape=jax.ShapeDtypeStruct((own,) + block, jnp.float32),
        in_specs=[pl.BlockSpec(memory_space=pl.ANY)] * 2,
        out_specs=pl.BlockSpec(memory_space=pltpu.VMEM),
        scratch_shapes=scratch
        + [
            pltpu.SemaphoreType.DMA((sems,)),
            pltpu.SemaphoreType.DMA((sems,)),
            pltpu.SemaphoreType.DMA((locals_,)),
        ],
        compiler_params=pltpu.CompilerParams(
            collective_id=3, has_side_effects=True, vmem_limit_bytes=VMEM_MAX
        ),
        name="scatter_sums",
    )(col_partial, row_partial)


def invert_panel(x):
    n = x.shape[0]
    rows = lax.broadcasted_iota(jnp.int32, (n, n), 0)
    cols = lax.broadcasted_iota(jnp.int32, (n, n), 1)
    pivots = jnp.ones((n, n), jnp.float32)
    group = 8
    for start in range(0, n, group):
        members = range(start, start + group)
        columns = {j: jnp.broadcast_to(x[:, j : j + 1], (n, n)) for j in members}
        for j in members:
            column = columns[j]
            pivot = column[j : j + 1, :]
            inverse = 1.0 / pivot
            below = jnp.where(rows > j, column, 0.0)
            for k in range(j + 1, start + group):
                factor = columns[k][j : j + 1, :] * inverse
                columns[k] = columns[k] - below * jnp.broadcast_to(factor, (n, n))
            line = jnp.where(cols[j : j + 1, :] == j, 1.0, x[j : j + 1, :]) * inverse
            pivots = jnp.where(rows == j, column, pivots)
            base = jnp.where(cols == j, jnp.where(rows == j, 1.0, 0.0), x)
            x = base - below * jnp.broadcast_to(line, (n, n))
    x = jnp.where(rows == cols, 1.0, jnp.where(rows > cols, x, 0.0))
    return x * lax.rsqrt(pivots)


def eliminate(panel, a_ref, out_ref):
    rank = a_ref.shape[0]
    out_ref[...] = a_ref[...]
    for k in range(rank // panel):
        lo, hi = k * panel, (k + 1) * panel
        inv = invert_panel(out_ref[lo:hi, lo:hi])
        out_ref[lo:hi, lo:hi] = inv
        strip = out_ref[lo:hi, :]
        cols = lax.broadcasted_iota(jnp.int32, strip.shape, 1)
        new = jnp.dot(inv, strip, precision=HIGHEST, preferred_element_type=jnp.float32)
        done = jnp.where((cols >= lo) & (cols < hi), strip, new)
        out_ref[lo:hi, :] = jnp.where(cols < hi, done, 0.0)
        if hi < rank:
            out_ref[hi:, lo:hi] = jnp.zeros((rank - hi, panel), jnp.float32)
            out_ref[hi:, :] -= lax.dot_general(
                new,
                done,
                (((0,), (0,)), ((), ())),
                precision=HIGHEST,
                preferred_element_type=jnp.float32,
            )[hi:, :]


def inverse_kernel(panel, near_identity, a_ref, out_ref):
    if not near_identity:
        eliminate(panel, a_ref, out_ref)
        return
    rows = lax.broadcasted_iota(jnp.int32, a_ref.shape, 0)
    cols = lax.broadcasted_iota(jnp.int32, a_ref.shape, 1)
    unit = jnp.where(rows == cols, 1.0, 0.0)

    def lower_half(e):
        return jnp.where(rows > cols, e, jnp.where(rows == cols, 0.5 * e, 0.0))

    def dot(x, y, contract):
        return lax.dot_general(
            x,
            y,
            (((1,), (contract,)), ((), ())),
            precision=HIGHEST,
            preferred_element_type=jnp.float32,
        )

    error = a_ref[...] - unit
    size = jnp.sum(error * error)
    near = size < 0.04

    @pl.when(jnp.logical_not(near))
    def _():
        eliminate(panel, a_ref, out_ref)

    @pl.when(near)
    def _():
        out_ref[...] = unit - lower_half(error)

        def more(carry):
            step, last = carry
            return (step < 4) & (last > 1e-9)

        def improve(carry):
            step, _ = carry
            w = out_ref[...]
            e = dot(dot(w, a_ref[...], 0), w, 1) - unit
            out_ref[...] = w - dot(lower_half(e), w, 0)
            return step + 1, jnp.sum(e * e)

        lax.while_loop(more, improve, (0, size))


def inverse_factor(a, near_identity=False):
    return pl.pallas_call(
        functools.partial(inverse_kernel, 32, near_identity),
        out_shape=jax.ShapeDtypeStruct(a.shape, jnp.float32),
        in_specs=[pl.BlockSpec(memory_space=pltpu.VMEM)],
        out_specs=pl.BlockSpec(memory_space=pltpu.VMEM),
        name="inverse_factor",
    )(a)


def times_transposed(x, m):
    return lax.dot_general(x, m, (((1,), (1,)), ((), ())), precision=HIGHEST)


def gram_of(x, y):
    return lax.dot_general(x, y, (((0,), (0,)), ((), ())), precision=HIGHEST)


def per_device(tile_list, tile_values, block_order, basis):
    rows_count = lax.axis_size("row")
    cols_count = lax.axis_size("col")
    own_blocks, edge, rank = basis.shape
    blocks_all = block_order.shape[0]
    scale = jnp.sqrt(jnp.float32(blocks_all * edge))
    row_here = lax.axis_index("row")
    row_group = own_blocks * cols_count
    present = tile_list[:, 0] >= 0
    slot_range = jnp.arange(blocks_all, dtype=jnp.int32)
    match = block_order[None, None, :] == tile_list[:, :, None]
    slots_both = jnp.sum(jnp.where(match, slot_range[None, None, :], 0), axis=2)
    first_slot = slots_both[:, 0]
    second_slot = slots_both[:, 1]
    row_local = jnp.where(present, first_slot - row_here * row_group, -1)
    owner_second = second_slot // own_blocks
    col_local = jnp.where(
        present, owner_second // cols_count * own_blocks + second_slot % own_blocks, -1
    )
    column_side, row_side = gather_sides(basis)
    row_partial, col_partial = tile_products(
        row_local, col_local, tile_values, column_side, row_side
    )
    product = scatter_sums(col_partial, row_partial, own_blocks).reshape(own_blocks * edge, rank)
    old = basis.reshape(own_blocks * edge, rank).astype(jnp.float32)
    sums = sum_all(gram_of(jnp.concatenate([product, old / scale], 1), product), 0)
    gram = sums[:rank]
    projected = sums[rank:]
    first_basis = times_transposed(product, inverse_factor(gram))
    second = sum_all(gram_of(first_basis, first_basis), 1)
    final = times_transposed(first_basis, inverse_factor(second, near_identity=True))
    basis_out = (final * scale).astype(jnp.bfloat16).reshape(own_blocks, edge, rank)
    return (basis_out, projected)


def solution(mesh):
    in_specs = (
        P(("row", "col"), None),
        P(("row", "col"), None, None),
        P(),
        P(("row", "col"), None, None),
    )
    out_specs = (P(("row", "col"), None, None), P())
    return jax.shard_map(
        per_device, mesh=mesh, in_specs=in_specs, out_specs=out_specs, check_vma=False
    )
```
